32 devices in a mesh: grp: 4 (over z), dev: 8 (over y, x, core).
Axes of the slice: x: 2, y: 2, z: 4, core: 2. Of those that a mesh axis runs over, the one named last changes fastest.
Arguments:
- sources: bfloat16 [8, 131072], P(None, ('grp', 'dev')), may hold values from -6 to 6
- boundary_impedance_input: float32 [8, 256], replicated, may hold values from -6 to 6
- leaf_inverse: bfloat16 [131072, 2048], P(('grp', 'dev')), may hold values from -0.1875 to 0.1875
- leaf_flux: bfloat16 [131072, 256], P(('grp', 'dev')), may hold values from -0.1875 to 0.1875
- leaf_lift: bfloat16 [16384, 2048], P(('grp', 'dev')), may hold values from -0.375 to 0.375
- node_schur: float32 [128, 64, 128], P(('grp', 'dev')), may hold values from -0.375 to 0.375
- node_spread: float32 [128, 64, 256], P(('grp', 'dev')), may hold values from -0.1875 to 0.1875
- node_lift: float32 [128, 128, 128], P(('grp', 'dev')), may hold values from -0.25 to 0.25
Outputs:
- field: float32 [8, 262144], P(None, ('grp', 'dev'))
The draws below stay inside these ranges and needn't reach their ends.
All inputs are finite; a program needn't handle non-finite values.
Results may differ from the reference program's by a relative error of at most 0.0025.
Values sent between devices are 32-bit elements; how exact they have to be, the bound alone decides.
A program may use at most 128 MiB of HBM per device.

```python
import jax
import jax.numpy as jnp
from jax import lax

SRC = 8
CELLS = 1024
EDGE = 128
IFACE = 64
LEAVES = 128


def block_levels(rng, extent, pieces, low, largest):
    def one(axis_at, blocks):
        draws = jax.random.uniform(jax.random.fold_in(jax.random.fold_in(rng, 6), axis_at), (blocks,), jnp.float32, low / len(pieces), largest / len(pieces))
        return jnp.repeat(jnp.exp(draws), extent[axis_at] // blocks).reshape((-1,) + (1,) * (len(extent) - axis_at - 1))

    level = one(*pieces[0])
    for cut in pieces[1:]:
        level = level * one(*cut)
    return level


def centred(key, dims, deviation, bound, shards=(), dtype=jnp.bfloat16):
    values = jax.random.normal(key, dims, jnp.float32) * deviation
    if len(shards) > 0:
        values = block_levels(key, dims, shards, -0.22, 0.18) * values
    return jnp.clip(values, min=-bound, max=bound).astype(dtype)


def setup_inputs(seed: int = 0) -> dict:
    key_list = jax.random.split(jax.random.key(seed), 9)
    sources = centred(key_list[0], (SRC, LEAVES * CELLS), 1.0, 6.0, ((1, 32),))
    boundary_impedance_input = centred(key_list[1], (SRC, 2 * EDGE), 1.0, 6.0, (), jnp.float32)
    leaf_inverse = centred(key_list[2], (LEAVES * CELLS, 2 * CELLS), CELLS ** -0.5, 0.1875, ((0, 32),))
    leaf_flux = centred(key_list[3], (LEAVES * CELLS, 2 * EDGE), CELLS ** -0.5, 0.1875, ((0, 32),))
    leaf_lift = centred(key_list[4], (LEAVES * EDGE, 2 * CELLS), (2 * EDGE) ** -0.5, 0.375, ((0, 32),))
    node_schur = centred(key_list[5], (LEAVES, IFACE, 2 * IFACE), (4 * IFACE) ** -0.5, 0.375, ((0, 32),), jnp.float32)
    node_spread = centred(key_list[6], (LEAVES, IFACE, 2 * EDGE), (16 * IFACE) ** -0.5, 0.1875, ((0, 32),), jnp.float32)
    node_lift = centred(key_list[7], (LEAVES, EDGE, 2 * IFACE), (4 * EDGE) ** -0.5, 0.25, ((0, 32),), jnp.float32)
    return dict(sources=sources, boundary_impedance_input=boundary_impedance_input, leaf_inverse=leaf_inverse, leaf_flux=leaf_flux, leaf_lift=leaf_lift, node_schur=node_schur, node_spread=node_spread, node_lift=node_lift)


def complex_mul(vector, matrix):
    inner = matrix.shape[1]
    cols = matrix.shape[2] // 2
    hp = lax.Precision.HIGHEST
    real_side = jnp.einsum('nsa,nab->nsb', vector[..., :inner], matrix[..., :cols], precision=hp) - jnp.einsum('nsa,nab->nsb', vector[..., inner:], matrix[..., cols:], precision=hp)
    imag_side = jnp.einsum('nsa,nab->nsb', vector[..., :inner], matrix[..., cols:], precision=hp) + jnp.einsum('nsa,nab->nsb', vector[..., inner:], matrix[..., :cols], precision=hp)
    return jnp.concatenate([real_side, imag_side], -1)


def select_component(vector, start, stop):
    half = vector.shape[-1] // 2
    return jnp.concatenate([vector[..., start:stop], vector[..., half + start:half + stop]], -1)


def join_parts(first, second):
    half_one = first.shape[-1] // 2
    half_two = second.shape[-1] // 2
    return jnp.concatenate([first[..., :half_one], second[..., :half_two], first[..., half_one:], second[..., half_two:]], -1)


def merge_pair(left_out, right_out, schur, spread):
    width = left_out.shape[-1] // 4
    jump = complex_mul(select_component(right_out, width, 2 * width) - select_component(left_out, width, 2 * width), schur)
    parent = join_parts(select_component(left_out, 0, width), select_component(right_out, 0, width)) + complex_mul(jump, spread)
    return jump, parent


def ascend(outgoing, schur, spread):
    levels = outgoing.shape[0].bit_length() - 1
    jumps = []
    for tier_index in range(levels):
        half_step = 2 ** tier_index
        jump, outgoing = merge_pair(outgoing[0::2], outgoing[1::2], schur[half_step::2 * half_step], spread[half_step::2 * half_step])
        jumps.append(jump)
    return outgoing, jumps


def descend(incoming, jumps, lift):
    for tier_index in reversed(range(len(jumps))):
        half_step = 2 ** tier_index
        width = incoming.shape[-1] // 4
        iface = complex_mul(incoming, lift[half_step::2 * half_step]) + jumps[tier_index]
        left_in = join_parts(select_component(incoming, 0, width), iface)
        right_in = join_parts(select_component(incoming, width, 2 * width), iface)
        incoming = jnp.stack([left_in, right_in], 1).reshape(-1, incoming.shape[1], incoming.shape[2])
    return incoming


def reference(sources, boundary_impedance_input, leaf_inverse, leaf_flux, leaf_lift, node_schur, node_spread, node_lift):
    source_blocks = sources.reshape(SRC, LEAVES, CELLS).transpose(1, 0, 2)
    flux = leaf_flux.reshape(LEAVES, CELLS, 2 * EDGE)

    def leaf_up(pair):
        return jnp.dot(pair[0], pair[1], preferred_element_type=jnp.float32)

    leaf_out = lax.map(leaf_up, (source_blocks, flux))
    top_out, jumps = ascend(leaf_out, node_schur, node_spread)
    incoming = descend(boundary_impedance_input[None], jumps, node_lift)
    leaf_input_values = incoming.astype(jnp.bfloat16)
    inverse = leaf_inverse.reshape(LEAVES, CELLS, 2 * CELLS)
    lifting_operator = leaf_lift.reshape(LEAVES, EDGE, 2 * CELLS)

    def leaf_down(items):
        block, data_in, inv_block, lift_block = items
        particular = jnp.dot(block, inv_block, preferred_element_type=jnp.float32)
        from_real = jnp.dot(data_in[:, :EDGE], lift_block, preferred_element_type=jnp.float32)
        from_imag = jnp.dot(data_in[:, EDGE:], lift_block, preferred_element_type=jnp.float32)
        lifted = jnp.concatenate([from_real[:, :CELLS] - from_imag[:, CELLS:], from_real[:, CELLS:] + from_imag[:, :CELLS]], 1)
        return particular + lifted

    field = lax.map(leaf_down, (source_blocks, leaf_input_values, inverse, lifting_operator))
    return field.transpose(1, 0, 2).reshape(SRC, LEAVES * 2 * CELLS)
```

```python
import functools

import jax
import jax.numpy as jnp
from jax import lax
from jax.experimental import pallas as pl
from jax.experimental.pallas import tpu as pltpu
from jax.sharding import PartitionSpec as P

MESH = pl.DeviceIdType.MESH
BF16 = jnp.bfloat16
F32 = jnp.float32


def dot(a, b):
    return jnp.dot(a, b, preferred_element_type=F32)


def split(x):
    hi = x.astype(BF16)
    return hi, (x - hi.astype(F32)).astype(BF16)


def combine(r, n):
    s = r.shape[0] // 2
    return jnp.concatenate([r[:s, :n] - r[s:, n:], r[s:, :n] + r[:s, n:]], 0)


def cmul(v, w):
    v_hi, v_lo = split(v)
    w_hi, w_lo = split(w)
    rows = v.shape[0]
    both = dot(jnp.concatenate([v_hi, v_lo], 0), w_hi)
    return combine(both[:rows] + both[rows:] + dot(v_hi, w_lo), w.shape[1] // 2)


def fold(x):
    n = x.shape[1] // 2
    return jnp.concatenate([x[:, :n], x[:, n:]], 0)


def join(a, b):
    return jnp.concatenate([a, b], 1)


def kernel(
    ng,
    nd,
    nl,
    src_ref,
    bnd_ref,
    inv_hbm,
    flux_hbm,
    ll_hbm,
    schur_hbm,
    spread_hbm,
    lift_hbm,
    out_ref,
    inv,
    flux,
    ll,
    fac_loc,
    fac_all,
    top,
    roots,
    groots,
    jump_loc,
    jump_all,
    jump_top,
    inv_sem,
    flux_sem,
    ll_sem,
    fl_sem,
    fa_sem,
    top_sem,
    fs_sem,
    fr_sem,
    bs_sem,
    br_sem,
    rs_sem,
    rr_sem,
    zs_sem,
    zr_sem,
    ws_sem,
    wr_sem,
    gs_sem,
    gr_sem,
):
    grp = lax.axis_index("grp")
    dev = lax.axis_index("dev")
    nc = nd // 2
    core = lax.rem(dev, 2)
    chip = dev // 2
    sib = chip * 2 + (1 - core)
    iface = schur_hbm.shape[1]
    edge = lift_hbm.shape[1]
    cells = inv.shape[0] // nl
    frows = fac_all.shape[1]
    half = frows // 2
    o_sp, o_im, o_li = iface, 2 * iface, 3 * iface

    flux_cp = [
        pltpu.make_async_copy(
            flux_hbm.at[pl.ds(l * cells, cells)], flux.at[pl.ds(l * cells, cells)], flux_sem.at[l]
        )
        for l in range(nl)
    ]
    def factor_copies(pick, dst, sems):
        parts = (
            (schur_hbm.at[pick], 0, iface),
            (spread_hbm.at[pick, :, pl.ds(0, edge)], o_sp, iface),
            (spread_hbm.at[pick, :, pl.ds(edge, edge)], o_im, iface),
            (lift_hbm.at[pick], o_li, edge),
        )
        return [
            pltpu.make_async_copy(ref, dst.at[pl.ds(off, rows)], sems.at[i])
            for i, (ref, off, rows) in enumerate(parts)
        ]

    fa_cp = factor_copies(0, fac_all.at[dev], fa_sem)
    fl_cp = [factor_copies(l, fac_loc.at[l], fl_sem.at[l]) for l in range(1, nl)]
    for cp in fa_cp + flux_cp:
        cp.start()
    for cps in fl_cp:
        for cp in cps:
            cp.start()

    barrier = pltpu.get_barrier_semaphore()
    for k in range(1, nd):
        pl.semaphore_signal(
            barrier, inc=1, device_id=(grp, lax.rem(dev + k, nd)), device_id_type=MESH
        )
    for k in range(1, ng):
        pl.semaphore_signal(
            barrier, inc=1, device_id=(lax.rem(grp + k, ng), dev), device_id_type=MESH
        )
    pl.semaphore_wait(barrier, nd - 1 + ng - 1)

    def remote(src, dst, ssem, rsem, g, d):
        return pltpu.make_async_remote_copy(
            src_ref=src, dst_ref=dst, send_sem=ssem, recv_sem=rsem,
            device_id=(g, d), device_id_type=MESH,
        )

    for cp in fa_cp:
        cp.wait()
    fac_send = [
        remote(
            fac_all.at[dev], fac_all.at[dev], fs_sem.at[k], fr_sem.at[k],
            grp, lax.rem(chip + k, nc) * 2 + core,
        )
        for k in range(1, nc)
    ]
    for cp in fac_send:
        cp.start()

    def pass_on(k):
        owner = lax.rem(chip + nc - k, nc) * 2 + core
        return remote(fac_all.at[owner], fac_all.at[owner], bs_sem.at[k], br_sem.at[k], grp, sib)

    fac_pass = [pass_on(k) for k in range(nc)]
    fac_pass[0].start()

    units = 2 * nl
    rows_u = cells // 2
    inv_cp = [
        pltpu.make_async_copy(
            inv_hbm.at[pl.ds(u * rows_u, rows_u)], inv.at[pl.ds(u * rows_u, rows_u)], inv_sem.at[u]
        )
        for u in range(units)
    ]
    ll_cp = pltpu.make_async_copy(ll_hbm, ll, ll_sem.at[0])

    for cp in flux_cp:
        cp.wait()
    for cp in inv_cp:
        cp.start()
    ll_cp.start()

    def merge(a, b, fac, jump_dst):
        diff = (b - a)[:, iface:]
        jump = cmul(diff, fac[0:iface, :])
        jump_dst[...] = jump
        spread = jnp.concatenate([fac[o_sp:o_im, :], fac[o_im:o_li, :]], 1)
        return join(a[:, :iface], b[:, :iface]) + cmul(jump, spread)

    def lower(inc, fac, jump):
        return cmul(inc, fac[o_li:frows, :]) + jump

    def climb(outs, fac_of, jump_of):
        half_step = 1
        while len(outs) > 1:
            outs = [
                merge(
                    outs[2 * i],
                    outs[2 * i + 1],
                    fac_of((2 * i + 1) * half_step),
                    jump_of((2 * i + 1) * half_step),
                )
                for i in range(len(outs) // 2)
            ]
            half_step *= 2
        return outs[0]

    outs = [
        fold(dot(src_ref[:, l * cells : (l + 1) * cells], flux[l * cells : (l + 1) * cells, :]))
        for l in range(nl)
    ]
    for cps in fl_cp:
        for cp in cps:
            cp.wait()
    roots[dev] = climb(outs, lambda s: fac_loc.at[s], lambda s: jump_loc.at[s])
    root_send = [
        remote(
            roots.at[dev], roots.at[dev], rs_sem.at[k], rr_sem.at[k], grp, lax.rem(dev + k, nd)
        )
        for k in range(1, nd)
    ]
    for cp in root_send:
        cp.start()

    width = 2 * cells

    def unit(u):
        inv_cp[u].wait()
        l = u // 2
        part = dot(
            src_ref[:, u * rows_u : (u + 1) * rows_u], inv[u * rows_u : (u + 1) * rows_u, :]
        )
        cols = slice(l * width, (l + 1) * width)
        if u % 2 == 0:
            out_ref[:, cols] = part
        else:
            out_ref[:, cols] += part

    def run_units(lo, hi):
        for u in range(lo, hi):
            unit(u)

    cut = [units * i // 8 for i in (0, 2, 3, 5, 8)]
    run_units(cut[0], cut[1])
    for k in range(1, nc):
        fac_send[k - 1].wait_recv()
        fac_pass[k].start()
    run_units(cut[1], cut[2])
    for cp in fac_pass:
        cp.wait_recv()
    rows_mine = pl.ds(pl.multiple_of(core * half, 8), half)
    top_own = pltpu.make_async_copy(fac_all.at[0], top.at[grp], top_sem.at[0])
    top_own.start()
    top_send = [
        remote(
            fac_all.at[0, rows_mine], top.at[grp, rows_mine], zs_sem.at[k], zr_sem.at[k],
            lax.rem(grp + k, ng), dev,
        )
        for k in range(1, ng)
    ]
    for cp in top_send:
        cp.start()

    for cp in root_send:
        cp.wait_recv()
    groots[grp] = climb(
        [roots[d] for d in range(nd)], lambda s: fac_all.at[s], lambda s: jump_all.at[s]
    )
    groot_send = [
        remote(
            groots.at[grp], groots.at[grp], gs_sem.at[k], gr_sem.at[k], lax.rem(grp + k, ng), dev
        )
        for k in range(1, ng)
    ]
    for cp in groot_send:
        cp.start()
    run_units(cut[2], cut[3])

    top_pass = []
    for k in range(1, ng):
        owner = lax.rem(grp + ng - k, ng)
        top_send[k - 1].wait_recv()
        cp = remote(
            top.at[owner, rows_mine], top.at[owner, rows_mine], ws_sem.at[k], wr_sem.at[k], grp, sib
        )
        cp.start()
        top_pass.append(cp)
    run_units(cut[3], cut[4])
    for cp in groot_send:
        cp.wait_recv()
    top_own.wait()
    for cp in top_pass:
        cp.wait_recv()
    climb([groots[g] for g in range(ng)], lambda s: top.at[s], lambda s: jump_top.at[s])

    inc = fold(bnd_ref[...])

    def follow(inc, place, count, fac, jumps):
        step = count // 2
        while step >= 1:
            s = (place // (2 * step)) * (2 * step) + step
            low = lower(inc, fac.at[s], jumps[s])
            right = lax.rem(place // step, 2) == 1
            inc = join(jnp.where(right, inc[:, iface:], inc[:, :iface]), low)
            step //= 2
        return inc

    inc = follow(inc, grp, ng, top, jump_top)
    inc = follow(inc, dev, nd, fac_all, jump_all)
    incs = [inc]
    step = nl // 2
    while step >= 1:
        below = []
        for i, inc in enumerate(incs):
            s = (2 * i + 1) * step
            low = lower(inc, fac_loc.at[s], jump_loc[s])
            below.append(join(inc[:, :iface], low))
            below.append(join(inc[:, iface:], low))
        incs = below
        step //= 2

    ll_cp.wait()
    for l in range(nl):
        lifted = dot(incs[l].astype(BF16), ll[l * edge : (l + 1) * edge, :])
        s = lifted.shape[0] // 2
        re = slice(l * width, l * width + cells)
        im = slice(l * width + cells, (l + 1) * width)
        out_ref[:, re] += lifted[:s, :cells] - lifted[s:, cells:]
        out_ref[:, im] += lifted[:s, cells:] + lifted[s:, :cells]

    for cp in fac_send + fac_pass + root_send + top_send + top_pass + groot_send:
        cp.wait_send()


def body(ng, nd, sources, boundary, inverse, flux, leaf_lift, schur, spread, lift):
    nl, iface = schur.shape[:2]
    edge = lift.shape[1]
    s = sources.shape[0]
    frows = 3 * iface + edge
    dma = pltpu.SemaphoreType.DMA
    nc = nd // 2
    vmem = pl.BlockSpec(memory_space=pltpu.VMEM)
    hbm = pl.BlockSpec(memory_space=pl.ANY)
    return pl.pallas_call(
        functools.partial(kernel, ng, nd, nl),
        out_shape=jax.ShapeDtypeStruct((s, nl * inverse.shape[1]), F32),
        in_specs=[vmem, vmem] + [hbm] * 6,
        out_specs=vmem,
        scratch_shapes=[
            pltpu.VMEM(inverse.shape, BF16),
            pltpu.VMEM(flux.shape, BF16),
            pltpu.VMEM(leaf_lift.shape, BF16),
            pltpu.VMEM((nl, frows, edge), F32),
            pltpu.VMEM((nd, frows, edge), F32),
            pltpu.VMEM((ng, frows, edge), F32),
            pltpu.VMEM((nd, 2 * s, edge), F32),
            pltpu.VMEM((ng, 2 * s, edge), F32),
            pltpu.VMEM((nl, 2 * s, iface), F32),
            pltpu.VMEM((nd, 2 * s, iface), F32),
            pltpu.VMEM((ng, 2 * s, iface), F32),
            dma((2 * nl,)),
            dma((nl,)),
            dma((1,)),
            dma((nl, 4)),
            dma((4,)),
            dma((1,)),
            dma((nc,)),
            dma((nc,)),
            dma((nc,)),
            dma((nc,)),
            dma((nd,)),
            dma((nd,)),
            dma((ng,)),
            dma((ng,)),
            dma((ng,)),
            dma((ng,)),
            dma((ng,)),
            dma((ng,)),
        ],
        compiler_params=pltpu.CompilerParams(
            collective_id=0, has_side_effects=True, vmem_limit_bytes=48 * 1024 * 1024
        ),
    )(sources, boundary, inverse, flux, leaf_lift, schur, spread, lift)


def solution(mesh):
    ng, nd = mesh.shape["grp"], mesh.shape["dev"]
    split_rows = P(("grp", "dev"), None)
    split_nodes = P(("grp", "dev"), None, None)
    in_specs = (
        P(None, ("grp", "dev")),
        P(),
        split_rows,
        split_rows,
        split_rows,
        split_nodes,
        split_nodes,
        split_nodes,
    )
    return jax.shard_map(
        functools.partial(body, ng, nd),
        mesh=mesh,
        in_specs=in_specs,
        out_specs=P(None, ("grp", "dev")),
        check_vma=False,
    )
```

```python
import functools
import math

import jax
import jax.numpy as jnp
from jax import lax
from jax.experimental import pallas as pl
from jax.experimental.pallas import tpu as pltpu
from jax.sharding import PartitionSpec as P

MESH = pl.DeviceIdType.MESH
BF16 = jnp.bfloat16
F32 = jnp.float32


def dot(a, b):
    return jnp.dot(a, b, preferred_element_type=F32)


def split(x):
    hi = x.astype(BF16)
    return hi, (x - hi.astype(F32)).astype(BF16)


def combine(r, n):
    s = r.shape[0] // 2
    return jnp.concatenate([r[:s, :n] - r[s:, n:], r[s:, :n] + r[:s, n:]], 0)


def cmul(v, w):
    v_hi, v_lo = split(v)
    w_hi, w_lo = split(w)
    rows = v.shape[0]
    both = dot(jnp.concatenate([v_hi, v_lo], 0), w_hi)
    return combine(both[:rows] + both[rows:] + dot(v_hi, w_lo), w.shape[1] // 2)


def fold(x):
    n = x.shape[1] // 2
    return jnp.concatenate([x[:, :n], x[:, n:]], 0)


def join(a, b):
    return jnp.concatenate([a, b], 1)


def kernel(
    ng,
    nd,
    nl,
    src_hbm,
    bnd_hbm,
    inv_hbm,
    flux_hbm,
    ll_hbm,
    schur_hbm,
    spread_hbm,
    lift_hbm,
    out_ref,
    src_ref,
    bnd_ref,
    inv,
    flux,
    ll,
    fac_loc,
    fac_all,
    top,
    pair,
    roots,
    groots,
    jump_loc,
    jump_all,
    jump_top,
    inv_sem,
    flux_sem,
    ll_sem,
    sb_sem,
    fl_sem,
    fa_sem,
    top_sem,
    fs_sem,
    fr_sem,
    bs_sem,
    br_sem,
    zs_sem,
    zr_sem,
    hs_sem,
    hr_sem,
    ws_sem,
    wr_sem,
    ps_sem,
    rs_sem,
    rr_sem,
    gs_sem,
    gr_sem,
):
    grp = lax.axis_index("grp")
    dev = lax.axis_index("dev")
    nc = nd // 2
    core = lax.rem(dev, 2)
    chip = dev // 2
    sib = chip * 2 + (1 - core)
    iface = schur_hbm.shape[1]
    edge = lift_hbm.shape[1]
    cells = inv.shape[0] // nl
    frows = fac_all.shape[1]
    npc = math.gcd(frows // 8, nc)
    piece = frows // npc
    o_sp, o_im, o_li = iface, 2 * iface, 3 * iface

    flux_cp = [
        pltpu.make_async_copy(
            flux_hbm.at[pl.ds(l * cells, cells)], flux.at[pl.ds(l * cells, cells)], flux_sem.at[l]
        )
        for l in range(nl)
    ]
    def factor_copies(pick, dst, sems):
        parts = (
            (schur_hbm.at[pick], 0, iface),
            (spread_hbm.at[pick, :, pl.ds(0, edge)], o_sp, iface),
            (spread_hbm.at[pick, :, pl.ds(edge, edge)], o_im, iface),
            (lift_hbm.at[pick], o_li, edge),
        )
        return [
            pltpu.make_async_copy(ref, dst.at[pl.ds(off, rows)], sems.at[i])
            for i, (ref, off, rows) in enumerate(parts)
        ]

    fa_cp = factor_copies(0, fac_all.at[dev], fa_sem)
    fl_cp = [factor_copies(l, fac_loc.at[l], fl_sem.at[l]) for l in range(1, nl)]
    src_cp = pltpu.make_async_copy(src_hbm, src_ref, sb_sem.at[0])
    bnd_cp = pltpu.make_async_copy(bnd_hbm, bnd_ref, sb_sem.at[1])
    for cp in fa_cp + [src_cp] + flux_cp + [bnd_cp]:
        cp.start()
    for cps in fl_cp:
        for cp in cps:
            cp.start()

    relay = jnp.logical_and(core == 0, chip < npc)
    barrier = pltpu.get_barrier_semaphore()
    for k in range(1, nd):
        pl.semaphore_signal(
            barrier, inc=1, device_id=(grp, lax.rem(dev + k, nd)), device_id_type=MESH
        )
    for k in range(1, ng):
        pl.semaphore_signal(
            barrier, inc=1, device_id=(lax.rem(grp + k, ng), dev), device_id_type=MESH
        )

    @pl.when(jnp.logical_and(relay, chip > 0))
    def _():
        for k in range(1, ng):
            pl.semaphore_signal(
                barrier, inc=1, device_id=(lax.rem(grp + k, ng), 0), device_id_type=MESH
            )

    @pl.when(dev == 0)
    def _():
        pl.semaphore_wait(barrier, nd - 1 + (ng - 1) * npc)

    @pl.when(dev != 0)
    def _():
        pl.semaphore_wait(barrier, nd - 1 + ng - 1)

    def remote(src, dst, ssem, rsem, g, d):
        return pltpu.make_async_remote_copy(
            src_ref=src, dst_ref=dst, send_sem=ssem, recv_sem=rsem,
            device_id=(g, d), device_id_type=MESH,
        )

    def same(ref, ssem, rsem, g, d):
        return remote(ref, ref, ssem, rsem, g, d)

    fac_send = [
        same(
            fac_all.at[dev], fs_sem.at[k], fr_sem.at[k], grp, lax.rem(chip + k, nc) * 2 + core
        )
        for k in range(1, nc)
    ]
    fac_pass = [
        same(
            fac_all.at[lax.rem(chip + nc - k, nc) * 2 + (core if k == 0 else 0)],
            bs_sem.at[k], br_sem.at[k], grp, sib,
        )
        for k in range(nc)
    ]
    deal = [
        remote(
            fac_all.at[0, pl.ds(c * piece, piece)], top.at[grp, pl.ds(c * piece, piece)],
            zs_sem.at[k, c], zr_sem.at[k], lax.rem(grp + k, ng), 2 * c,
        )
        for k in range(1, ng)
        for c in range(npc)
    ]
    mine = pl.ds(pl.multiple_of(chip * piece, 8), piece)

    def other(k):
        return lax.rem(grp + ng - k, ng)

    deal_in = [
        same(top.at[other(k), mine], zs_sem.at[k, 0], zr_sem.at[k], grp, sib)
        for k in range(1, ng)
    ]
    spread_out = [
        [
            same(
                top.at[other(k), mine], hs_sem.at[k, j], hr_sem.at[k, j],
                grp, lax.rem(chip + j, nc) * 2,
            )
            for j in range(1, nc)
        ]
        for k in range(1, ng)
    ]
    top_pass = [
        same(top.at[other(k)], ws_sem.at[k], wr_sem.at[k], grp, sib) for k in range(1, ng)
    ]

    for cp in fa_cp:
        cp.wait()

    fac_pass[0].start()

    @pl.when(core == 0)
    def _():
        for cp in fac_send:
            cp.start()

    @pl.when(dev == 0)
    def _():
        for cp in deal:
            cp.start()

    units = 2 * nl
    rows_u = cells // 2
    inv_cp = [
        pltpu.make_async_copy(
            inv_hbm.at[pl.ds(u * rows_u, rows_u)], inv.at[pl.ds(u * rows_u, rows_u)], inv_sem.at[u]
        )
        for u in range(units)
    ]
    ll_cp = pltpu.make_async_copy(ll_hbm, ll, ll_sem.at[0])

    for cp in [src_cp] + flux_cp:
        cp.wait()
    for cp in inv_cp:
        cp.start()
    ll_cp.start()

    def merge(a, b, fac, jump_dst):
        diff = (b - a)[:, iface:]
        jump = cmul(diff, fac[0:iface, :])
        jump_dst[...] = jump
        spread = jnp.concatenate([fac[o_sp:o_im, :], fac[o_im:o_li, :]], 1)
        return join(a[:, :iface], b[:, :iface]) + cmul(jump, spread)

    def lower(inc, fac, jump):
        return cmul(inc, fac[o_li:frows, :]) + jump

    def climb(outs, fac_of, jump_of):
        half_step = 1
        while len(outs) > 1:
            outs = [
                merge(
                    outs[2 * i],
                    outs[2 * i + 1],
                    fac_of((2 * i + 1) * half_step),
                    jump_of((2 * i + 1) * half_step),
                )
                for i in range(len(outs) // 2)
            ]
            half_step *= 2
        return outs[0]

    outs = [
        fold(dot(src_ref[:, l * cells : (l + 1) * cells], flux[l * cells : (l + 1) * cells, :]))
        for l in range(nl)
    ]
    for cps in fl_cp:
        for cp in cps:
            cp.wait()
    pair[core] = climb(outs, lambda s: fac_loc.at[s], lambda s: jump_loc.at[s])
    pair_send = same(pair.at[core], ps_sem.at[0], ps_sem.at[1], grp, sib)
    pair_send.start()

    width = 2 * cells

    def unit(u):
        inv_cp[u].wait()
        l = u // 2
        part = dot(
            src_ref[:, u * rows_u : (u + 1) * rows_u], inv[u * rows_u : (u + 1) * rows_u, :]
        )
        cols = slice(l * width, (l + 1) * width)
        if u % 2 == 0:
            out_ref[:, cols] = part
        else:
            out_ref[:, cols] += part

    def run_units(lo, hi):
        for u in range(lo, hi):
            unit(u)

    cut = [units * i // 8 for i in (0, 2, 4, 6, 8)]
    run_units(cut[0], cut[1])
    fac_pass[0].wait_recv()
    pair_send.wait_recv()
    odd = chip * 2 + 1
    roots[chip] = merge(pair[0], pair[1], fac_all.at[odd], jump_all.at[odd])
    root_send = [
        same(roots.at[chip], rs_sem.at[k], rr_sem.at[k], grp, lax.rem(chip + k, nc) * 2 + core)
        for k in range(1, nc)
    ]
    for cp in root_send:
        cp.start()

    @pl.when(core == 0)
    def _():
        for k in range(1, nc):
            fac_send[k - 1].wait_recv()
            fac_pass[k].start()

    @pl.when(relay)
    def _():
        for k in range(1, ng):
            deal_in[k - 1].wait_recv()
            for cp in spread_out[k - 1]:
                cp.start()

    run_units(cut[1], cut[2])

    @pl.when(core == 1)
    def _():
        for k in range(1, nc):
            fac_pass[k].wait_recv()

    top_own = pltpu.make_async_copy(fac_all.at[0], top.at[grp], top_sem.at[0])
    top_own.start()
    for cp in root_send:
        cp.wait_recv()
    groots[grp] = climb(
        [roots[c] for c in range(nc)], lambda s: fac_all.at[2 * s], lambda s: jump_all.at[2 * s]
    )
    groot_send = [
        same(groots.at[grp], gs_sem.at[k], gr_sem.at[k], lax.rem(grp + k, ng), dev)
        for k in range(1, ng)
    ]
    for cp in groot_send:
        cp.start()
    run_units(cut[2], cut[3])

    @pl.when(core == 0)
    def _():
        for k in range(1, ng):
            for j in range(1, nc):
                from_chip = lax.rem(chip + nc - j, nc)

                def got(k=k, j=j):
                    spread_out[k - 1][j - 1].wait_recv()

                if npc == nc:
                    got()
                else:
                    pl.when(from_chip < npc)(got)
            top_pass[k - 1].start()

    run_units(cut[3], cut[4])
    for cp in groot_send:
        cp.wait_recv()
    top_own.wait()

    @pl.when(core == 1)
    def _():
        for cp in top_pass:
            cp.wait_recv()

    climb([groots[g] for g in range(ng)], lambda s: top.at[s], lambda s: jump_top.at[s])

    bnd_cp.wait()
    inc = fold(bnd_ref[...])

    def follow(inc, place, count, fac, jumps):
        step = count // 2
        while step >= 1:
            s = (place // (2 * step)) * (2 * step) + step
            low = lower(inc, fac.at[s], jumps[s])
            right = lax.rem(place // step, 2) == 1
            inc = join(jnp.where(right, inc[:, iface:], inc[:, :iface]), low)
            step //= 2
        return inc

    inc = follow(inc, grp, ng, top, jump_top)
    inc = follow(inc, dev, nd, fac_all, jump_all)
    incs = [inc]
    step = nl // 2
    while step >= 1:
        below = []
        for i, inc in enumerate(incs):
            s = (2 * i + 1) * step
            low = lower(inc, fac_loc.at[s], jump_loc[s])
            below.append(join(inc[:, :iface], low))
            below.append(join(inc[:, iface:], low))
        incs = below
        step //= 2

    ll_cp.wait()
    for l in range(nl):
        lifted = dot(incs[l].astype(BF16), ll[l * edge : (l + 1) * edge, :])
        s = lifted.shape[0] // 2
        re = slice(l * width, l * width + cells)
        im = slice(l * width + cells, (l + 1) * width)
        out_ref[:, re] += lifted[:s, :cells] - lifted[s:, cells:]
        out_ref[:, im] += lifted[:s, cells:] + lifted[s:, :cells]

    for cp in [fac_pass[0], pair_send] + root_send + groot_send:
        cp.wait_send()

    @pl.when(core == 0)
    def _():
        for cp in fac_send + fac_pass[1:] + top_pass:
            cp.wait_send()

    @pl.when(relay)
    def _():
        for cps in spread_out:
            for cp in cps:
                cp.wait_send()

    @pl.when(dev == 0)
    def _():
        for cp in deal:
            cp.wait_send()


def body(ng, nd, sources, boundary, inverse, flux, leaf_lift, schur, spread, lift):
    nl, iface = schur.shape[:2]
    edge = lift.shape[1]
    s = sources.shape[0]
    frows = 3 * iface + edge
    dma = pltpu.SemaphoreType.DMA
    nc = nd // 2
    vmem = pl.BlockSpec(memory_space=pltpu.VMEM)
    hbm = pl.BlockSpec(memory_space=pltpu.MemorySpace.HBM)
    return pl.pallas_call(
        functools.partial(kernel, ng, nd, nl),
        out_shape=jax.ShapeDtypeStruct((s, nl * inverse.shape[1]), F32),
        in_specs=[hbm] * 8,
        out_specs=vmem,
        scratch_shapes=[
            pltpu.VMEM(sources.shape, BF16),
            pltpu.VMEM(boundary.shape, F32),
            pltpu.VMEM(inverse.shape, BF16),
            pltpu.VMEM(flux.shape, BF16),
            pltpu.VMEM(leaf_lift.shape, BF16),
            pltpu.VMEM((nl, frows, edge), F32),
            pltpu.VMEM((nd, frows, edge), F32),
            pltpu.VMEM((ng, frows, edge), F32),
            pltpu.VMEM((2, 2 * s, edge), F32),
            pltpu.VMEM((nc, 2 * s, edge), F32),
            pltpu.VMEM((ng, 2 * s, edge), F32),
            pltpu.VMEM((nl, 2 * s, iface), F32),
            pltpu.VMEM((nd, 2 * s, iface), F32),
            pltpu.VMEM((ng, 2 * s, iface), F32),
            dma((2 * nl,)),
            dma((nl,)),
            dma((1,)),
            dma((2,)),
            dma((nl, 4)),
            dma((4,)),
            dma((1,)),
            dma((nc,)),
            dma((nc,)),
            dma((nc,)),
            dma((nc,)),
            dma((ng, nc)),
            dma((ng,)),
            dma((ng, nc)),
            dma((ng, nc)),
            dma((ng,)),
            dma((ng,)),
            dma((2,)),
            dma((nc,)),
            dma((nc,)),
            dma((ng,)),
            dma((ng,)),
        ],
        compiler_params=pltpu.CompilerParams(
            collective_id=0, has_side_effects=True, vmem_limit_bytes=63 * 1024 * 1024
        ),
    )(sources, boundary, inverse, flux, leaf_lift, schur, spread, lift)


def solution(mesh):
    ng, nd = mesh.shape["grp"], mesh.shape["dev"]
    split_rows = P(("grp", "dev"), None)
    split_nodes = P(("grp", "dev"), None, None)
    in_specs = (
        P(None, ("grp", "dev")),
        P(),
        split_rows,
        split_rows,
        split_rows,
        split_nodes,
        split_nodes,
        split_nodes,
    )
    return jax.shard_map(
        functools.partial(body, ng, nd),
        mesh=mesh,
        in_specs=in_specs,
        out_specs=P(None, ("grp", "dev")),
        check_vma=False,
    )
```

```python
import functools
import math

import jax
import jax.numpy as jnp
from jax import lax
from jax.experimental import pallas as pl
from jax.experimental.pallas import tpu as pltpu
from jax.sharding import PartitionSpec as P

MESH = pl.DeviceIdType.MESH
BF16 = jnp.bfloat16
F32 = jnp.float32


def dot(a, b):
    return jnp.dot(a, b, preferred_element_type=F32)


def split(x):
    hi = x.astype(BF16)
    return hi, (x - hi.astype(F32)).astype(BF16)


def combine(r, n):
    s = r.shape[0] // 2
    return jnp.concatenate([r[:s, :n] - r[s:, n:], r[s:, :n] + r[:s, n:]], 0)


def cmul(v, w):
    v_hi, v_lo = split(v)
    w_hi, w_lo = split(w)
    rows = v.shape[0]
    both = dot(jnp.concatenate([v_hi, v_lo], 0), w_hi)
    return combine(both[:rows] + both[rows:] + dot(v_hi, w_lo), w.shape[1] // 2)


def fold(x):
    n = x.shape[1] // 2
    return jnp.concatenate([x[:, :n], x[:, n:]], 0)


def join(a, b):
    return jnp.concatenate([a, b], 1)


def kernel(
    ng,
    nd,
    nl,
    src_hbm,
    bnd_hbm,
    inv_hbm,
    flux_hbm,
    ll_hbm,
    schur_hbm,
    spread_hbm,
    lift_hbm,
    out_ref,
    src_ref,
    bnd_ref,
    inv,
    flux,
    ll,
    fac_loc,
    fac_all,
    top,
    pair,
    roots,
    groots,
    jump_loc,
    jump_all,
    jump_top,
    inv_sem,
    flux_sem,
    ll_sem,
    sb_sem,
    fl_sem,
    fa_sem,
    top_sem,
    fs_sem,
    fr_sem,
    bs_sem,
    br_sem,
    zs_sem,
    zr_sem,
    hs_sem,
    hr_sem,
    ws_sem,
    wr_sem,
    ps_sem,
    rs_sem,
    rr_sem,
    gs_sem,
    gr_sem,
):
    grp = lax.axis_index("grp")
    dev = lax.axis_index("dev")
    nc = nd // 2
    core = lax.rem(dev, 2)
    chip = dev // 2
    sib = chip * 2 + (1 - core)
    iface = schur_hbm.shape[1]
    edge = lift_hbm.shape[1]
    cells = inv.shape[0] // nl
    frows = fac_all.shape[1]
    npc = math.gcd(frows // 8, nc)
    piece = frows // npc
    o_sp, o_im, o_li = iface, 2 * iface, 3 * iface

    flux_cp = [
        pltpu.make_async_copy(
            flux_hbm.at[pl.ds(l * cells, cells)], flux.at[pl.ds(l * cells, cells)], flux_sem.at[l]
        )
        for l in range(nl)
    ]
    def factor_copies(pick, dst, sems):
        parts = (
            (schur_hbm.at[pick], 0, iface),
            (spread_hbm.at[pick, :, pl.ds(0, edge)], o_sp, iface),
            (spread_hbm.at[pick, :, pl.ds(edge, edge)], o_im, iface),
            (lift_hbm.at[pick], o_li, edge),
        )
        return [
            pltpu.make_async_copy(ref, dst.at[pl.ds(off, rows)], sems.at[i])
            for i, (ref, off, rows) in enumerate(parts)
        ]

    fa_cp = factor_copies(0, fac_all.at[dev], fa_sem)
    fl_cp = [factor_copies(l, fac_loc.at[l], fl_sem.at[l]) for l in range(1, nl)]
    src_cp = pltpu.make_async_copy(src_hbm, src_ref, sb_sem.at[0])
    bnd_cp = pltpu.make_async_copy(bnd_hbm, bnd_ref, sb_sem.at[1])
    for cp in fa_cp + [src_cp] + flux_cp + [bnd_cp]:
        cp.start()
    for cps in fl_cp:
        for cp in cps:
            cp.start()

    relay = jnp.logical_and(core == 0, chip < npc)
    barrier = pltpu.get_barrier_semaphore()
    for k in range(1, nd):
        pl.semaphore_signal(
            barrier, inc=1, device_id=(grp, lax.rem(dev + k, nd)), device_id_type=MESH
        )
    for k in range(1, ng):
        pl.semaphore_signal(
            barrier, inc=1, device_id=(lax.rem(grp + k, ng), dev), device_id_type=MESH
        )

    @pl.when(jnp.logical_and(relay, chip > 0))
    def _():
        for k in range(1, ng):
            pl.semaphore_signal(
                barrier, inc=1, device_id=(lax.rem(grp + k, ng), 0), device_id_type=MESH
            )

    units = 2 * nl
    rows_u = cells // 2
    inv_cp = [
        pltpu.make_async_copy(
            inv_hbm.at[pl.ds(u * rows_u, rows_u)], inv.at[pl.ds(u * rows_u, rows_u)], inv_sem.at[u]
        )
        for u in range(units)
    ]
    ll_cp = pltpu.make_async_copy(ll_hbm, ll, ll_sem.at[0])

    for cp in [src_cp] + flux_cp:
        cp.wait()
    for cp in inv_cp:
        cp.start()
    ll_cp.start()

    def merge(a, b, fac, jump_dst):
        diff = (b - a)[:, iface:]
        jump = cmul(diff, fac[0:iface, :])
        jump_dst[...] = jump
        spread = jnp.concatenate([fac[o_sp:o_im, :], fac[o_im:o_li, :]], 1)
        return join(a[:, :iface], b[:, :iface]) + cmul(jump, spread)

    def lower(inc, fac, jump):
        return cmul(inc, fac[o_li:frows, :]) + jump

    def climb(outs, fac_of, jump_of):
        half_step = 1
        while len(outs) > 1:
            outs = [
                merge(
                    outs[2 * i],
                    outs[2 * i + 1],
                    fac_of((2 * i + 1) * half_step),
                    jump_of((2 * i + 1) * half_step),
                )
                for i in range(len(outs) // 2)
            ]
            half_step *= 2
        return outs[0]

    outs = [
        fold(dot(src_ref[:, l * cells : (l + 1) * cells], flux[l * cells : (l + 1) * cells, :]))
        for l in range(nl)
    ]
    for cps in fl_cp:
        for cp in cps:
            cp.wait()
    pair[core] = climb(outs, lambda s: fac_loc.at[s], lambda s: jump_loc.at[s])
    @pl.when(dev == 0)
    def _():
        pl.semaphore_wait(barrier, nd - 1 + (ng - 1) * npc)

    @pl.when(dev != 0)
    def _():
        pl.semaphore_wait(barrier, nd - 1 + ng - 1)

    def remote(src, dst, ssem, rsem, g, d):
        return pltpu.make_async_remote_copy(
            src_ref=src, dst_ref=dst, send_sem=ssem, recv_sem=rsem,
            device_id=(g, d), device_id_type=MESH,
        )

    def same(ref, ssem, rsem, g, d):
        return remote(ref, ref, ssem, rsem, g, d)

    fac_send = [
        same(
            fac_all.at[dev], fs_sem.at[k], fr_sem.at[k], grp, lax.rem(chip + k, nc) * 2 + core
        )
        for k in range(1, nc)
    ]
    fac_pass = [
        same(
            fac_all.at[lax.rem(chip + nc - k, nc) * 2 + (core if k == 0 else 0)],
            bs_sem.at[k], br_sem.at[k], grp, sib,
        )
        for k in range(nc)
    ]
    deal = [
        remote(
            fac_all.at[0, pl.ds(c * piece, piece)], top.at[grp, pl.ds(c * piece, piece)],
            zs_sem.at[k, c], zr_sem.at[k], lax.rem(grp + k, ng), 2 * c,
        )
        for k in range(1, ng)
        for c in range(npc)
    ]
    mine = pl.ds(pl.multiple_of(chip * piece, 8), piece)

    def other(k):
        return lax.rem(grp + ng - k, ng)

    deal_in = [
        same(top.at[other(k), mine], zs_sem.at[k, 0], zr_sem.at[k], grp, sib)
        for k in range(1, ng)
    ]
    spread_out = [
        [
            same(
                top.at[other(k), mine], hs_sem.at[k, j], hr_sem.at[k, j],
                grp, lax.rem(chip + j, nc) * 2,
            )
            for j in range(1, nc)
        ]
        for k in range(1, ng)
    ]
    top_pass = [
        same(top.at[other(k)], ws_sem.at[k], wr_sem.at[k], grp, sib) for k in range(1, ng)
    ]

    for cp in fa_cp:
        cp.wait()

    fac_pass[0].start()

    @pl.when(core == 0)
    def _():
        for cp in fac_send:
            cp.start()

    @pl.when(jnp.logical_and(dev == 0, grp > 0))
    def _():
        for cp in deal:
            cp.start()

    pair_send = same(pair.at[core], ps_sem.at[0], ps_sem.at[1], grp, sib)
    pair_send.start()

    width = 2 * cells

    def unit(u):
        inv_cp[u].wait()
        l = u // 2
        part = dot(
            src_ref[:, u * rows_u : (u + 1) * rows_u], inv[u * rows_u : (u + 1) * rows_u, :]
        )
        cols = slice(l * width, (l + 1) * width)
        if u % 2 == 0:
            out_ref[:, cols] = part
        else:
            out_ref[:, cols] += part

    def run_units(lo, hi):
        for u in range(lo, hi):
            unit(u)

    cut = [units * i // 8 for i in (0, 2, 4, 6, 8)]
    run_units(cut[0], cut[1])
    fac_pass[0].wait_recv()
    pair_send.wait_recv()
    odd = chip * 2 + 1
    roots[chip] = merge(pair[0], pair[1], fac_all.at[odd], jump_all.at[odd])
    root_send = [
        same(roots.at[chip], rs_sem.at[k], rr_sem.at[k], grp, lax.rem(chip + k, nc) * 2 + core)
        for k in range(1, nc)
    ]
    for cp in root_send:
        cp.start()

    @pl.when(core == 0)
    def _():
        for k in range(1, nc):
            fac_send[k - 1].wait_recv()
            fac_pass[k].start()

    @pl.when(relay)
    def _():
        for k in range(1, ng):

            @pl.when(other(k) > 0)
            def _(k=k):
                deal_in[k - 1].wait_recv()
                for cp in spread_out[k - 1]:
                    cp.start()

    run_units(cut[1], cut[2])

    @pl.when(core == 1)
    def _():
        for k in range(1, nc):
            fac_pass[k].wait_recv()

    top_own = pltpu.make_async_copy(fac_all.at[0], top.at[grp], top_sem.at[0])
    top_own.start()
    for cp in root_send:
        cp.wait_recv()
    groots[grp] = climb(
        [roots[c] for c in range(nc)], lambda s: fac_all.at[2 * s], lambda s: jump_all.at[2 * s]
    )
    groot_send = [
        same(groots.at[grp], gs_sem.at[k], gr_sem.at[k], lax.rem(grp + k, ng), dev)
        for k in range(1, ng)
    ]
    for cp in groot_send:
        cp.start()
    run_units(cut[2], cut[3])

    @pl.when(core == 0)
    def _():
        for k in range(1, ng):
            for j in range(1, nc):
                from_chip = lax.rem(chip + nc - j, nc)

                def got(k=k, j=j):
                    spread_out[k - 1][j - 1].wait_recv()

                pl.when(jnp.logical_and(from_chip < npc, other(k) > 0))(got)
            pl.when(other(k) > 0)(top_pass[k - 1].start)

    run_units(cut[3], cut[4])
    for cp in groot_send:
        cp.wait_recv()
    top_own.wait()

    @pl.when(core == 1)
    def _():
        for k in range(1, ng):
            pl.when(other(k) > 0)(top_pass[k - 1].wait_recv)

    climb([groots[g] for g in range(ng)], lambda s: top.at[s], lambda s: jump_top.at[s])

    bnd_cp.wait()
    inc = fold(bnd_ref[...])

    def follow(inc, place, count, fac, jumps):
        step = count // 2
        while step >= 1:
            s = (place // (2 * step)) * (2 * step) + step
            low = lower(inc, fac.at[s], jumps[s])
            right = lax.rem(place // step, 2) == 1
            inc = join(jnp.where(right, inc[:, iface:], inc[:, :iface]), low)
            step //= 2
        return inc

    inc = follow(inc, grp, ng, top, jump_top)
    inc = follow(inc, dev, nd, fac_all, jump_all)
    incs = [inc]
    step = nl // 2
    while step >= 1:
        below = []
        for i, inc in enumerate(incs):
            s = (2 * i + 1) * step
            low = lower(inc, fac_loc.at[s], jump_loc[s])
            below.append(join(inc[:, :iface], low))
            below.append(join(inc[:, iface:], low))
        incs = below
        step //= 2

    ll_cp.wait()
    for l in range(nl):
        lifted = dot(incs[l].astype(BF16), ll[l * edge : (l + 1) * edge, :])
        s = lifted.shape[0] // 2
        re = slice(l * width, l * width + cells)
        im = slice(l * width + cells, (l + 1) * width)
        out_ref[:, re] += lifted[:s, :cells] - lifted[s:, cells:]
        out_ref[:, im] += lifted[:s, cells:] + lifted[s:, :cells]

    for cp in [fac_pass[0], pair_send] + root_send + groot_send:
        cp.wait_send()

    @pl.when(core == 0)
    def _():
        for cp in fac_send + fac_pass[1:]:
            cp.wait_send()
        for k in range(1, ng):
            pl.when(other(k) > 0)(top_pass[k - 1].wait_send)

    @pl.when(relay)
    def _():
        for k in range(1, ng):

            @pl.when(other(k) > 0)
            def _(k=k):
                for cp in spread_out[k - 1]:
                    cp.wait_send()

    @pl.when(jnp.logical_and(dev == 0, grp > 0))
    def _():
        for cp in deal:
            cp.wait_send()


def body(ng, nd, sources, boundary, inverse, flux, leaf_lift, schur, spread, lift):
    nl, iface = schur.shape[:2]
    edge = lift.shape[1]
    s = sources.shape[0]
    frows = 3 * iface + edge
    dma = pltpu.SemaphoreType.DMA
    nc = nd // 2
    vmem = pl.BlockSpec(memory_space=pltpu.VMEM)
    hbm = pl.BlockSpec(memory_space=pltpu.MemorySpace.HBM)
    return pl.pallas_call(
        functools.partial(kernel, ng, nd, nl),
        out_shape=jax.ShapeDtypeStruct((s, nl * inverse.shape[1]), F32),
        in_specs=[hbm] * 8,
        out_specs=vmem,
        scratch_shapes=[
            pltpu.VMEM(sources.shape, BF16),
            pltpu.VMEM(boundary.shape, F32),
            pltpu.VMEM(inverse.shape, BF16),
            pltpu.VMEM(flux.shape, BF16),
            pltpu.VMEM(leaf_lift.shape, BF16),
            pltpu.VMEM((nl, frows, edge), F32),
            pltpu.VMEM((nd, frows, edge), F32),
            pltpu.VMEM((ng, frows, edge), F32),
            pltpu.VMEM((2, 2 * s, edge), F32),
            pltpu.VMEM((nc, 2 * s, edge), F32),
            pltpu.VMEM((ng, 2 * s, edge), F32),
            pltpu.VMEM((nl, 2 * s, iface), F32),
            pltpu.VMEM((nd, 2 * s, iface), F32),
            pltpu.VMEM((ng, 2 * s, iface), F32),
            dma((2 * nl,)),
            dma((nl,)),
            dma((1,)),
            dma((2,)),
            dma((nl, 4)),
            dma((4,)),
            dma((1,)),
            dma((nc,)),
            dma((nc,)),
            dma((nc,)),
            dma((nc,)),
            dma((ng, nc)),
            dma((ng,)),
            dma((ng, nc)),
            dma((ng, nc)),
            dma((ng,)),
            dma((ng,)),
            dma((2,)),
            dma((nc,)),
            dma((nc,)),
            dma((ng,)),
            dma((ng,)),
        ],
        compiler_params=pltpu.CompilerParams(
            collective_id=0, has_side_effects=True, vmem_limit_bytes=63 * 1024 * 1024
        ),
    )(sources, boundary, inverse, flux, leaf_lift, schur, spread, lift)


def solution(mesh):
    ng, nd = mesh.shape["grp"], mesh.shape["dev"]
    split_rows = P(("grp", "dev"), None)
    split_nodes = P(("grp", "dev"), None, None)
    in_specs = (
        P(None, ("grp", "dev")),
        P(),
        split_rows,
        split_rows,
        split_rows,
        split_nodes,
        split_nodes,
        split_nodes,
    )
    return jax.shard_map(
        functools.partial(body, ng, nd),
        mesh=mesh,
        in_specs=in_specs,
        out_specs=P(None, ("grp", "dev")),
        check_vma=False,
    )
```
